32 devices in a mesh: wide: 4 (over z), band: 8 (over y, x, core).
Axes of the slice: x: 2, y: 2, z: 4, core: 2. Of those that a mesh axis runs over, the one named last changes fastest.
Arguments:
- day_field: float32 [64, 128, 512], P('wide', 'band'), may hold values from -6 to 6
- obs_mask: int32 [64, 128, 512], P(None, 'band', 'wide'), may hold values 0 or 1
- ocean_mask: int32 [128, 512], P('band', 'wide'), may hold values 0 or 1
- diffusivity: float32 [128, 512], P('band', 'wide'), may hold values from 0.05 to 0.24
- start_modes: float32 [64, 48], replicated, may hold values from -6 to 6
Outputs:
- filled: float32 [64, 128, 512], P(None, 'band', 'wide')
- mode_basis: float32 [64, 48], replicated
The draws below stay inside these ranges and needn't reach their ends.
All inputs are finite; a program needn't handle non-finite values. No bound on the sum of `obs_mask` or of `ocean_mask` on one device may be relied on, other than what follows from the above.
Results may differ from the reference program's by a relative error of at most 0.00024.
Values sent between devices are 32-bit elements; how exact they have to be, the bound alone decides.
No kernel may reach another device: no remote copies, remote signals or barrier semaphores. Data moves between devices by JAX's collectives and lax.ppermute only.
A program may use at most 64 MiB of HBM per device.

```python
import math
import jax
import jax.numpy as jnp
from jax import lax

DAYS = 64
MODES = 48
OUTER = 3
INNER = 3
PASSES = 3
LAT = 128
LON = 512


def touch_ends(values, stream_key, least, high):
    longest = values.shape.index(max(values.shape))
    spots = []
    for shift in (0, 1):
        where = [jax.random.randint(jax.random.fold_in(stream_key, axis), (), 0, length) for axis, length in enumerate(values.shape)]
        where[longest] = (where[longest] + shift) % values.shape[longest]
        spots.append(tuple(where))
    return values.at[spots[0]].set(least).at[spots[1]].set(high)


def level_of(key, extent, split, smallest, top_value):
    def one(dim, shards_of):
        draws = jax.random.uniform(jax.random.fold_in(jax.random.fold_in(key, 6), dim), (shards_of,), jnp.float32, smallest / len(split), top_value / len(split))
        return jnp.repeat(jnp.exp(draws), extent[dim] // shards_of).reshape((-1,) + (1,) * (len(extent) - dim - 1))

    level = one(*split[0])
    for cut in split[1:]:
        level = level * one(*cut)
    return level


def bell_draw(own_key, extent, width, reach, cuts=(), held_as=jnp.bfloat16):
    level = level_of(own_key, extent, cuts, -0.22, 0.18) if cuts else 1.0
    values = jax.random.normal(own_key, extent, jnp.float32) * width * level
    return jnp.minimum(jnp.maximum(values, -reach), reach).astype(held_as)


def setup_inputs(seed: int = 0) -> dict:
    splits = jax.random.split(jax.random.key(seed), 6)
    return {
        "day_field": bell_draw(splits[0], (DAYS, LAT, LON), 1.0, 6.0, ((0, 4), (1, 8)), jnp.float32),
        "obs_mask": touch_ends((jax.random.randint(splits[1], (DAYS, LAT, LON), 0, 2) < 1).astype(jnp.int32), jax.random.fold_in(splits[1], 1), 0, 1),
        "ocean_mask": touch_ends((jax.random.randint(splits[2], (LAT, LON), 0, 5) < 4).astype(jnp.int32), jax.random.fold_in(splits[2], 1), 0, 1),
        "diffusivity": jnp.clip(jnp.exp(math.log(0.24) - 1.5686159 * jax.random.uniform(splits[3], (LAT, LON), jnp.float32) ** level_of(splits[3], (LAT, LON), ((0, 8), (1, 4)), -0.2, 0.2)), 0.05, 0.24),
        "start_modes": bell_draw(splits[4], (DAYS, MODES), 1.0, 6.0, (), jnp.float32),
    }


def orthonormal(coeff):
    gram_matrix = jnp.dot(coeff.T.astype(jnp.float32), coeff.astype(jnp.float32), precision=lax.Precision.HIGHEST, preferred_element_type=jnp.float32)
    factor = jnp.linalg.cholesky(gram_matrix)
    return jax.scipy.linalg.solve_triangular(factor, coeff.T, lower=True).T

def laplace(values):
    padded = jnp.pad(values, ((0, 0), (1, 1), (0, 0)))
    return padded[:, 2:] + padded[:, :-2] + jnp.roll(values, 1, 2) + jnp.roll(values, -1, 2) - 4.0 * values

def contract_pixels(left, right):
    return lax.dot_general(left.astype(jnp.float32), right.astype(jnp.float32), (((1,), (1,)), ((), ())), precision=lax.Precision.HIGHEST, preferred_element_type=jnp.float32)

def reference(day_field, obs_mask, ocean_mask, diffusivity, start_modes):
    ocean_wide = ocean_mask[None]
    valid = (obs_mask * ocean_wide).astype(jnp.float32)
    gap_weight = ((1 - obs_mask) * ocean_wide).astype(jnp.float32)
    gap_coef = diffusivity[None] * gap_weight
    observed = day_field * valid
    mode_basis = orthonormal(start_modes)
    filled = observed
    for outer_step in range(OUTER):
        flat_field = filled.reshape(DAYS, LAT * LON)
        for inner_step in range(INNER):
            projected = jnp.dot(mode_basis.T.astype(jnp.float32), flat_field.astype(jnp.float32), precision=lax.Precision.HIGHEST, preferred_element_type=jnp.float32)
            mode_basis = orthonormal(contract_pixels(flat_field, projected))
        projected = jnp.dot(mode_basis.T.astype(jnp.float32), flat_field.astype(jnp.float32), precision=lax.Precision.HIGHEST, preferred_element_type=jnp.float32)
        recon = jnp.dot(mode_basis.astype(jnp.float32), projected.astype(jnp.float32), precision=lax.Precision.HIGHEST, preferred_element_type=jnp.float32)
        filled = observed + gap_weight * recon.reshape(DAYS, LAT, LON)
        for pass_index in range(PASSES):
            filled = filled + gap_coef * laplace(filled)
    return (filled, mode_basis)
```

```python
import functools
import jax
import jax.numpy as jnp
from jax import lax
from jax.experimental import pallas as pl
from jax.experimental.pallas import tpu as pltpu
from jax.sharding import PartitionSpec as P

OUTER = 3
INNER = 3
PASSES = 3
HALO = OUTER * PASSES
LANES = 128
EXTRA = 8
FLOOR = 0.02

F32 = jnp.float32
BF16 = jnp.bfloat16
VMEM = pl.BlockSpec(memory_space=pltpu.VMEM)
SMEM = pl.BlockSpec(memory_space=pltpu.SMEM)


def highest(left, right, left_dim, right_dim):
    return lax.dot_general(
        left,
        right,
        (((left_dim,), (right_dim,)), ((), ())),
        precision=lax.Precision.HIGHEST,
        preferred_element_type=F32,
    )


def halves(value):
    high = value.astype(BF16)
    return high, (value - high.astype(F32)).astype(BF16)


def thirds(value):
    first = value.astype(BF16)
    rest = value - first.astype(F32)
    second = rest.astype(BF16)
    return first, second, (rest - second.astype(F32)).astype(BF16)


def grid_of(shape, axis):
    return lax.broadcasted_iota(jnp.int32, shape, axis)


def covariance_of(rows_of, count):
    days = None
    total = None
    for start in range(0, count, 2):
        pair = jnp.concatenate([rows_of(start), rows_of(start + 1)], axis=1)
        days = pair.shape[0]
        stack = jnp.concatenate(thirds(pair), axis=0)
        part = lax.dot_general(
            stack, stack, (((1,), (1,)), ((), ())), preferred_element_type=F32
        )
        total = part if total is None else total + part
    block = lambda i, j: total[i * days : (i + 1) * days, j * days : (j + 1) * days]
    small = block(2, 2) + (block(1, 2) + block(2, 1))
    small = small + (block(0, 2) + block(2, 0)) + block(1, 1)
    return block(0, 0) + ((block(0, 1) + block(1, 0)) + small)


def pack_symmetric(packed_ref, cov):
    half = cov.shape[0] // 2
    quarter = half // 2
    upper = grid_of((half, half), 1) >= grid_of((half, half), 0)
    same = grid_of((half, half), 1) == grid_of((half, half), 0)
    low = cov[half:, half:]
    mixed = jnp.where(upper, cov[:half, :half], low)
    cross = cov[:half, half:]
    body = jnp.concatenate(
        [mixed[:quarter], cross[:quarter], mixed[quarter:], cross[quarter:]], axis=1
    )
    diagonal = jnp.sum(jnp.where(same, low, 0.0), axis=0, keepdims=True)
    diagonal = jnp.concatenate([diagonal, jnp.zeros((1, LANES - half), F32)], axis=1)
    each = quarter // 2
    for side in range(2):
        for row in range(each):
            packed_ref[side, :, row * LANES : (row + 1) * LANES] = body[
                side * each + row : side * each + row + 1
            ]
        packed_ref[side, :, each * LANES :] = (
            diagonal if side == 0 else jnp.zeros((1, LANES), F32)
        )


def unpack_symmetric(parts_ref, body_ref, days):
    half = days // 2
    quarter = half // 2
    each = quarter // 2
    sides = []
    for side in range(2):
        values = [parts_ref[j] for j in range(side, parts_ref.shape[0], 2)]
        while len(values) > 1:
            paired = [values[i] + values[i + 1] for i in range(0, len(values) - 1, 2)]
            values = paired + values[len(paired) * 2 :]
        sides.append(values[0])
        for row in range(each):
            body_ref[side * each + row : side * each + row + 1, :] = values[0][
                :, row * LANES : (row + 1) * LANES
            ]
    body = body_ref[...]
    diagonal = sides[0][:, each * LANES : each * LANES + half]
    mixed = jnp.concatenate([body[:, :half], body[:, 2 * half : 3 * half]], axis=0)
    cross = jnp.concatenate([body[:, half : 2 * half], body[:, 3 * half :]], axis=0)
    col, row = grid_of((half, half), 1), grid_of((half, half), 0)
    flipped = mixed.T
    high = jnp.where(col >= row, mixed, flipped)
    low = jnp.where(col < row, mixed, flipped)
    low = jnp.where(col == row, jnp.broadcast_to(diagonal, (half, half)), low)
    top = jnp.concatenate([high, cross], axis=1)
    bottom = jnp.concatenate([cross.T, low], axis=1)
    return jnp.concatenate([top, bottom], axis=0)


def orthonormal_rows(rows):
    count, width = rows.shape
    gram = highest(rows, rows, 1, 1)
    pad = jnp.zeros((count, LANES - count - width), F32)
    table = jnp.concatenate([gram, rows, pad], axis=1)
    groups = [table[8 * i : 8 * i + 8] for i in range(count // 8)]
    sublane = grid_of((8, LANES), 0)
    pivots = []
    spread = lambda row: jnp.broadcast_to(row, (8, LANES))
    for k in range(0, count, 2):
        i, s = k // 8, k % 8
        first = [jnp.broadcast_to(g[:, k : k + 1], (8, LANES)) for g in groups[i:]]
        second = [jnp.broadcast_to(g[:, k + 1 : k + 2], (8, LANES)) for g in groups[i:]]
        row0, row1 = spread(groups[i][s : s + 1]), spread(groups[i][s + 1 : s + 2])
        a = spread(first[0][s : s + 1])
        b = spread(first[0][s + 1 : s + 2])
        c = spread(second[0][s + 1 : s + 2])
        det = a * c - b * b
        scale = 1.0 / det
        h0, h1, h2 = c * scale, b * scale, a * scale
        w0 = h0 * row0 - h1 * row1
        w1 = h2 * row1 - h1 * row0
        ratio = b / a
        pivots.append((a, c - b * ratio))
        for j in range(i, len(groups)):
            c0, c1 = first[j - i], second[j - i]
            updated = groups[j] - (c0 * w0 + c1 * w1)
            if j == i:
                updated = jnp.where(sublane > s + 1, updated, groups[j])
                updated = jnp.where(sublane == s + 1, row1 - ratio * row0, updated)
            groups[j] = updated
    outs, worst = [], None
    for i, g in enumerate(groups):
        d = jnp.zeros((8, LANES), F32)
        for s in range(8):
            d = jnp.where(sublane == s, pivots[(8 * i + s) // 2][s % 2], d)
        own = grid_of((8, LANES), 1) == sublane + 8 * i
        start = jnp.sum(
            jnp.where(own, table[8 * i : 8 * i + 8], 0.0), axis=1, keepdims=True
        )
        kept = d / start
        worst = kept if worst is None else jnp.minimum(worst, kept)
        outs.append(g[:, count : count + width] * lax.rsqrt(d)[:, :width])
    return jnp.concatenate(outs, axis=0), jnp.min(worst)


def start_kernel(modes_ref, rows_ref):
    rows_ref[...], _ = orthonormal_rows(modes_ref[...].T)


def modes_kernel(parts_ref, rows_ref, new_ref, last_ref, body_ref):
    rows = rows_ref[...]
    days = rows.shape[1]
    cov = unpack_symmetric(parts_ref, body_ref, days)
    same = grid_of((days, days), 1) == grid_of((days, days), 0)
    peak = jnp.max(jnp.where(same, cov, 0.0), keepdims=True)
    cov = cov * (1.0 / peak)
    moved = highest(rows, cov, 1, 0)
    twice = highest(cov, cov, 1, 0)
    new, kept = orthonormal_rows(highest(moved, twice, 1, 0))
    new_ref[...] = new

    @pl.when(jnp.logical_not(kept >= FLOOR))
    def _():
        def step(_, held):
            return orthonormal_rows(highest(held, cov, 1, 0))[0]

        new_ref[...] = lax.fori_loop(0, INNER, step, rows)

    final = new_ref[...]
    last_ref[...] = highest(final, final, 0, 0)


def static_kernel(obs_ref, ocean_ref, diff_ref, stat_ref):
    days, rows, cols = obs_ref.shape
    flat = obs_ref.reshape(days * rows, cols)
    for r in range(rows):
        seen = flat[pl.ds(r, days, stride=rows), :]
        ocean = ocean_ref[r : r + 1, :]
        stat_ref[r, :days, :] = ((1 - seen) * ocean).astype(F32)
        rest = jnp.concatenate(
            [
                diff_ref[r : r + 1, :],
                ocean.astype(F32),
                jnp.zeros((EXTRA - 2, cols), F32),
            ],
            axis=0,
        )
        stat_ref[r, days:, :] = rest


def observed_kernel(blocks, offs_ref, *refs):
    piece_refs = refs[:blocks]
    stat_ref, seen_ref, packed_ref = refs[blocks:]
    rows, days, cols = seen_ref.shape
    each = piece_refs[0].shape[0]
    for r in range(rows):
        ocean = stat_ref[r, days + 1 : days + 2, :]
        for b, piece_ref in enumerate(piece_refs):
            flat = piece_ref.reshape(each * rows, cols)
            start = pl.multiple_of(offs_ref[b], each)
            gap = stat_ref[r, pl.ds(start, each), :]
            value = flat[pl.ds(r, each, stride=rows), :]
            seen_ref[r, pl.ds(start, each), :] = value * (ocean - gap)
    pack_symmetric(packed_ref, covariance_of(lambda r: seen_ref[r], rows))


def row_source(refs, rows, e):
    north, main, south = refs
    if e < HALO:
        return north[e]
    if e < HALO + rows:
        return main[e - HALO]
    return south[e - HALO - rows]


def strip_kernel(*refs):
    seen, stat = refs[0:3], refs[3:6]
    east_ref, west_ref = refs[6:]
    rows, days, cols = seen[1].shape
    per = cols // HALO
    lane_seen = grid_of((days, cols), 1)
    lane_stat = grid_of((days + EXTRA, cols), 1)
    total = rows + 2 * HALO
    for tile in range(east_ref.shape[0]):
        for source, at, lane in (
            (seen, slice(0, days), lane_seen),
            (stat, slice(days, None), lane_stat),
        ):
            east = jnp.zeros(lane.shape, F32)
            west = jnp.zeros(lane.shape, F32)
            for j in range(min(per, total - tile * per)):
                value = row_source(source, rows, tile * per + j)
                here = (lane >= j * HALO) & (lane < (j + 1) * HALO)
                to_west = pltpu.roll(value, j * HALO, 1) if j else value
                to_east = pltpu.roll(value, (j + 1) * HALO, 1)
                west = jnp.where(here, to_west, west)
                east = jnp.where(here, to_east, east)
            east_ref[tile, at, :] = east
            west_ref[tile, at, :] = west


def project_rows(last, f_ref, out_ref, seen_ref, gap_ref, low, high):
    p0, p1 = halves(last)
    weights = jnp.concatenate([p0, p0, p1, p1], axis=1)

    def row(e, _):
        f0, f1 = halves(f_ref[e])
        stack = jnp.concatenate([f0, f1, f0, f1], axis=0)
        recon = jnp.dot(weights, stack, preferred_element_type=F32)
        out_ref[e] = seen_ref[e] + gap_ref[e] * recon
        return 0

    lax.fori_loop(low, high, row, 0)


def smooth_rows(f_ref, out_ref, gap_ref, diff_ref, low, high):
    width = f_ref.shape[2]

    def row(e, _):
        value = f_ref[e]
        around = f_ref[e - 1] + f_ref[e + 1]
        around = around + pltpu.roll(value, 1, 1) + pltpu.roll(value, width - 1, 1)
        coef = gap_ref[e] * diff_ref[e]
        out_ref[e] = value + coef * (around - 4.0 * value)
        return 0

    lax.fori_loop(low, high, row, 0)


def sweep_body(sweep, last, f_ref, a_ref, b_ref, seen_ref, gap_ref, diff_ref):
    total = seen_ref.shape[0]
    edge = sweep * PASSES
    project_rows(last, f_ref, a_ref, seen_ref, gap_ref, edge, total - edge)
    now, other = a_ref, b_ref
    for step in range(PASSES):
        edge += 1
        smooth_rows(now, other, gap_ref, diff_ref, edge, total - edge)
        now, other = other, now
    return now


def first_kernel(*refs):
    last_ref = refs[0]
    seen, stat = refs[1:4], refs[4:7]
    east_ref, west_ref = refs[7:9]
    seen_ref, gap_ref, diff_ref, out_ref, packed_ref = refs[9:14]
    a_ref = refs[14]
    rows, days, cols = seen[1].shape
    total = rows + 2 * HALO
    per = cols // HALO
    lane = grid_of((days, cols), 1)
    lane1 = grid_of((1, cols), 1)

    def side(e, at, lane):
        tile, j = e // per, e % per
        east, west = east_ref[tile, at, :], west_ref[tile, at, :]
        shift = (cols - j * HALO) % cols
        east = pltpu.roll(east, shift, 1) if shift else east
        west = pltpu.roll(west, cols - (j + 1) * HALO, 1)
        value = jnp.where(lane >= cols - HALO, west, 0.0)
        return jnp.where(lane < HALO, east, value)

    for e in range(total):
        seen_ref[e, :, :cols] = row_source(seen, rows, e)
        seen_ref[e, :, cols:] = side(e, slice(0, days), lane)
        whole = row_source(stat, rows, e)
        gap_ref[e, :, :cols] = whole[:days]
        gap_ref[e, :, cols:] = side(e, slice(days, 2 * days), lane)
        diff_ref[e, :, :cols] = whole[days : days + 1]
        diff_ref[e, :, cols:] = side(e, slice(2 * days, 2 * days + 1), lane1)
    now = sweep_body(
        0, last_ref[...], seen_ref, a_ref, out_ref, seen_ref, gap_ref, diff_ref
    )
    assert now is out_ref
    cov = covariance_of(lambda r: out_ref[HALO + r, :, :cols], rows)
    pack_symmetric(packed_ref, cov)


def next_kernel(sweep, last_ref, f_ref, seen_ref, gap_ref, diff_ref, out_ref, packed_ref, a_ref):
    now = sweep_body(sweep, last_ref[...], f_ref, a_ref, out_ref, seen_ref, gap_ref, diff_ref)
    assert now is out_ref
    rows = out_ref.shape[0] - 2 * HALO
    cols = out_ref.shape[2] // 2
    cov = covariance_of(lambda r: out_ref[HALO + r, :, :cols], rows)
    pack_symmetric(packed_ref, cov)


def end_kernel(sweep, last_ref, f_ref, seen_ref, gap_ref, diff_ref, rows_ref, out_ref, modes_ref, a_ref, b_ref):
    now = sweep_body(sweep, last_ref[...], f_ref, a_ref, b_ref, seen_ref, gap_ref, diff_ref)
    days, rows, cols = out_ref.shape
    flat = out_ref.reshape(days * rows, cols)
    for r in range(rows):
        flat[pl.ds(r, days, stride=rows), :] = now[HALO + r, :, :cols]
    modes_ref[...] = rows_ref[...].T


def call(kernel, name, ins, outs, scratch=(), scalars=0):
    specs = [SMEM] * scalars + [VMEM] * (len(ins) - scalars)
    return pl.pallas_call(
        kernel,
        name=name,
        out_shape=[jax.ShapeDtypeStruct(s, F32) for s in outs],
        in_specs=specs,
        out_specs=[VMEM] * len(outs),
        scratch_shapes=[pltpu.VMEM(s, F32) for s in scratch],
        compiler_params=pltpu.CompilerParams(vmem_limit_bytes=24 * 2**20),
    )(*ins)


def sum_parts(packed):
    count = lax.axis_size("band")
    width = packed.shape[2]
    parity = lax.rem(lax.axis_index("band"), 2)
    mine = lax.dynamic_slice_in_dim(packed, parity, 1, 0)
    other = lax.dynamic_slice_in_dim(packed, 1 - parity, 1, 0)
    got = lax.ppermute(other, "band", [(i, i ^ 1) for i in range(count)])
    everyone = count * lax.axis_size("wide")
    copies = jnp.broadcast_to(mine + got, (everyone, 1, width))
    return lax.all_to_all(copies, ("wide", "band"), 0, 0, tiled=True)


def edges(cells):
    rows = cells.shape[0]
    count = lax.axis_size("band")
    north = lax.ppermute(cells[rows - HALO :], "band", [(i, i + 1) for i in range(count - 1)])
    south = lax.ppermute(cells[:HALO], "band", [(i + 1, i) for i in range(count - 1)])
    return [north, cells, south]


def shards(day_field, obs_mask, ocean_mask, diffusivity, start_modes):
    days, rows, cols = obs_mask.shape
    modes = start_modes.shape[1]
    count = lax.axis_size("wide")
    me = lax.axis_index("wide")
    pieces, offs = [], []
    for k in range(count):
        to = lambda i: i ^ k
        piece = lax.dynamic_slice_in_dim(day_field, to(me) * cols, cols, 2)
        if k:
            piece = lax.ppermute(piece, "wide", [(i, to(i)) for i in range(count)])
        pieces.append(piece)
        offs.append(to(me) * day_field.shape[0])
    (stat,) = call(
        static_kernel, "static", [obs_mask, ocean_mask, diffusivity], [(rows, days + EXTRA, cols)]
    )
    stats = edges(stat)
    (basis,) = call(start_kernel, "start", [start_modes], [(modes, days)])
    offs = jnp.stack(offs).astype(jnp.int32)
    width = (days // 8 // 2 * 2 // 2 // 2 * 2 + 1) * LANES
    width = (days // 8 + 1) * LANES
    seen, packed = call(
        functools.partial(observed_kernel, count),
        "observed",
        [offs] + pieces + [stat],
        [(rows, days, cols), (2, 1, width)],
        scalars=1,
    )
    seens = edges(seen)
    parts = sum_parts(packed)
    total = rows + 2 * HALO
    tiles = pl.cdiv(total, cols // HALO)
    strip = (tiles, 2 * days + EXTRA, cols)
    east, west = call(strip_kernel, "strips", seens + stats, [strip, strip])
    from_west = lax.ppermute(east, "wide", [(i, (i + 1) % count) for i in range(count)])
    from_east = lax.ppermute(west, "wide", [((i + 1) % count, i) for i in range(count)])
    quarter = (days // 4, LANES)
    orth = lambda parts, basis: call(
        modes_kernel, "modes", [parts, basis], [(modes, days), (days, days)], [quarter]
    )
    wide_map, wide_row = (total, days, 2 * cols), (total, 1, 2 * cols)
    basis, last = orth(parts, basis)
    seen_w, gap_w, diff_w, filled, packed = call(
        first_kernel,
        "sweep0",
        [last] + seens + stats + [from_east, from_west],
        [wide_map, wide_map, wide_row, wide_map, (2, 1, width)],
        [wide_map],
    )
    for sweep in range(1, OUTER):
        basis, last = orth(sum_parts(packed), basis)
        ins = [last, filled, seen_w, gap_w, diff_w]
        if sweep < OUTER - 1:
            filled, packed = call(
                functools.partial(next_kernel, sweep),
                f"sweep{sweep}",
                ins,
                [wide_map, (2, 1, width)],
                [wide_map],
            )
        else:
            out, mode_basis = call(
                functools.partial(end_kernel, sweep),
                f"sweep{sweep}",
                ins + [basis],
                [(days, rows, cols), (days, modes)],
                [wide_map, wide_map],
            )
    return (out, mode_basis)


def solution(mesh):
    placed = (
        P("wide", "band", None),
        P(None, "band", "wide"),
        P("band", "wide"),
        P("band", "wide"),
        P(),
    )
    return jax.shard_map(
        shards,
        mesh=mesh,
        in_specs=placed,
        out_specs=(P(None, "band", "wide"), P()),
        check_vma=False,
    )
```

```python
import functools
import jax
import jax.numpy as jnp
from jax import lax
from jax.experimental import pallas as pl
from jax.experimental.pallas import tpu as pltpu
from jax.sharding import PartitionSpec as P

OUTER = 3
INNER = 3
PASSES = 3
HALO = OUTER * PASSES
LANES = 128
EXTRA = 8
CHUNK = 8
BATCH = 2
FLOOR = 0.02

F32 = jnp.float32
BF16 = jnp.bfloat16
VMEM = pl.BlockSpec(memory_space=pltpu.VMEM)
SMEM = pl.BlockSpec(memory_space=pltpu.SMEM)


def highest(left, right, left_dim, right_dim):
    return lax.dot_general(
        left,
        right,
        (((left_dim,), (right_dim,)), ((), ())),
        precision=lax.Precision.HIGHEST,
        preferred_element_type=F32,
    )


def halves(value):
    high = value.astype(BF16)
    return high, (value - high.astype(F32)).astype(BF16)


def thirds(value):
    first = value.astype(BF16)
    rest = value - first.astype(F32)
    second = rest.astype(BF16)
    return first, second, (rest - second.astype(F32)).astype(BF16)


def grid_of(shape, axis):
    return lax.broadcasted_iota(jnp.int32, shape, axis)


def covariance_of(rows_of, count):
    days = None
    total = None
    for start in range(0, count, 2):
        pair = jnp.concatenate([rows_of(start), rows_of(start + 1)], axis=1)
        days = pair.shape[0]
        stack = jnp.concatenate(thirds(pair), axis=0)
        part = lax.dot_general(
            stack, stack, (((1,), (1,)), ((), ())), preferred_element_type=F32
        )
        total = part if total is None else total + part
    block = lambda i, j: total[i * days : (i + 1) * days, j * days : (j + 1) * days]
    small = block(2, 2) + (block(1, 2) + block(2, 1))
    small = small + (block(0, 2) + block(2, 0)) + block(1, 1)
    return block(0, 0) + ((block(0, 1) + block(1, 0)) + small)


def pack_symmetric(packed_ref, cov):
    half = cov.shape[0] // 2
    quarter = half // 2
    upper = grid_of((half, half), 1) >= grid_of((half, half), 0)
    same = grid_of((half, half), 1) == grid_of((half, half), 0)
    low = cov[half:, half:]
    mixed = jnp.where(upper, cov[:half, :half], low)
    cross = cov[:half, half:]
    body = jnp.concatenate(
        [mixed[:quarter], cross[:quarter], mixed[quarter:], cross[quarter:]], axis=1
    )
    diagonal = jnp.sum(jnp.where(same, low, 0.0), axis=0, keepdims=True)
    diagonal = jnp.concatenate([diagonal, jnp.zeros((1, LANES - half), F32)], axis=1)
    each = quarter // 2
    for side in range(2):
        for row in range(each):
            packed_ref[side, :, row * LANES : (row + 1) * LANES] = body[
                side * each + row : side * each + row + 1
            ]
        packed_ref[side, :, each * LANES :] = (
            diagonal if side == 0 else jnp.zeros((1, LANES), F32)
        )


def unpack_symmetric(parts_ref, body_ref, days):
    half = days // 2
    quarter = half // 2
    each = quarter // 2
    sides = []
    for side in range(2):
        values = [parts_ref[j] for j in range(side, parts_ref.shape[0], 2)]
        while len(values) > 1:
            paired = [values[i] + values[i + 1] for i in range(0, len(values) - 1, 2)]
            values = paired + values[len(paired) * 2 :]
        sides.append(values[0])
        for row in range(each):
            body_ref[side * each + row : side * each + row + 1, :] = values[0][
                :, row * LANES : (row + 1) * LANES
            ]
    body = body_ref[...]
    diagonal = sides[0][:, each * LANES : each * LANES + half]
    mixed = jnp.concatenate([body[:, :half], body[:, 2 * half : 3 * half]], axis=0)
    cross = jnp.concatenate([body[:, half : 2 * half], body[:, 3 * half :]], axis=0)
    col, row = grid_of((half, half), 1), grid_of((half, half), 0)
    flipped = mixed.T
    high = jnp.where(col >= row, mixed, flipped)
    low = jnp.where(col < row, mixed, flipped)
    low = jnp.where(col == row, jnp.broadcast_to(diagonal, (half, half)), low)
    top = jnp.concatenate([high, cross], axis=1)
    bottom = jnp.concatenate([cross.T, low], axis=1)
    return jnp.concatenate([top, bottom], axis=0)


def orthonormal_rows(rows):
    count, width = rows.shape
    gram = highest(rows, rows, 1, 1)
    pad = jnp.zeros((count, LANES - count - width), F32)
    table = jnp.concatenate([gram, rows, pad], axis=1)
    groups = [table[8 * i : 8 * i + 8] for i in range(count // 8)]
    sublane = grid_of((8, LANES), 0)
    pivots = []
    spread = lambda row: jnp.broadcast_to(row, (8, LANES))
    for k in range(0, count, 2):
        i, s = k // 8, k % 8
        first = [jnp.broadcast_to(g[:, k : k + 1], (8, LANES)) for g in groups[i:]]
        second = [jnp.broadcast_to(g[:, k + 1 : k + 2], (8, LANES)) for g in groups[i:]]
        row0, row1 = spread(groups[i][s : s + 1]), spread(groups[i][s + 1 : s + 2])
        a = spread(first[0][s : s + 1])
        b = spread(first[0][s + 1 : s + 2])
        c = spread(second[0][s + 1 : s + 2])
        det = a * c - b * b
        scale = 1.0 / det
        h0, h1, h2 = c * scale, b * scale, a * scale
        w0 = h0 * row0 - h1 * row1
        w1 = h2 * row1 - h1 * row0
        ratio = b / a
        pivots.append((a, c - b * ratio))
        for j in range(i, len(groups)):
            c0, c1 = first[j - i], second[j - i]
            updated = groups[j] - (c0 * w0 + c1 * w1)
            if j == i:
                updated = jnp.where(sublane > s + 1, updated, groups[j])
                updated = jnp.where(sublane == s + 1, row1 - ratio * row0, updated)
            groups[j] = updated
    outs, worst = [], None
    for i, g in enumerate(groups):
        d = jnp.zeros((8, LANES), F32)
        for s in range(8):
            d = jnp.where(sublane == s, pivots[(8 * i + s) // 2][s % 2], d)
        own = grid_of((8, LANES), 1) == sublane + 8 * i
        start = jnp.sum(
            jnp.where(own, table[8 * i : 8 * i + 8], 0.0), axis=1, keepdims=True
        )
        kept = d / start
        worst = kept if worst is None else jnp.minimum(worst, kept)
        outs.append(g[:, count : count + width] * lax.rsqrt(d)[:, :width])
    return jnp.concatenate(outs, axis=0), jnp.min(worst)


def start_kernel(modes_ref, rows_ref):
    rows_ref[...], _ = orthonormal_rows(modes_ref[...].T)


def modes_kernel(parts_ref, rows_ref, new_ref, last_ref, body_ref):
    rows = rows_ref[...]
    days = rows.shape[1]
    cov = unpack_symmetric(parts_ref, body_ref, days)
    same = grid_of((days, days), 1) == grid_of((days, days), 0)
    peak = jnp.max(jnp.where(same, cov, 0.0), keepdims=True)
    cov = cov * (1.0 / peak)
    moved = highest(rows, cov, 1, 0)
    twice = highest(cov, cov, 1, 0)
    new, kept = orthonormal_rows(highest(moved, twice, 1, 0))
    new_ref[...] = new

    @pl.when(jnp.logical_not(kept >= FLOOR))
    def _():
        def step(_, held):
            return orthonormal_rows(highest(held, cov, 1, 0))[0]

        new_ref[...] = lax.fori_loop(0, INNER, step, rows)

    final = new_ref[...]
    last_ref[...] = highest(final, final, 0, 0)


def static_kernel(obs_ref, ocean_ref, diff_ref, stat_ref):
    days, rows, cols = obs_ref.shape
    flat = obs_ref.reshape(days * rows, cols)
    for r in range(rows):
        seen = flat[pl.ds(r, days, stride=rows), :]
        ocean = ocean_ref[r : r + 1, :]
        stat_ref[r, :days, :] = ((1 - seen) * ocean).astype(F32)
        rest = jnp.concatenate(
            [
                diff_ref[r : r + 1, :],
                ocean.astype(F32),
                jnp.zeros((EXTRA - 2, cols), F32),
            ],
            axis=0,
        )
        stat_ref[r, days:, :] = rest


def observed_kernel(blocks, offs_ref, *refs):
    piece_refs = refs[:blocks]
    stat_ref, seen_ref, packed_ref = refs[blocks:]
    rows, days, cols = seen_ref.shape
    each = piece_refs[0].shape[0]
    for r in range(rows):
        ocean = stat_ref[r, days + 1 : days + 2, :]
        for b, piece_ref in enumerate(piece_refs):
            flat = piece_ref.reshape(each * rows, cols)
            start = pl.multiple_of(offs_ref[b], each)
            gap = stat_ref[r, pl.ds(start, each), :]
            value = flat[pl.ds(r, each, stride=rows), :]
            seen_ref[r, pl.ds(start, each), :] = value * (ocean - gap)
    pack_symmetric(packed_ref, covariance_of(lambda r: seen_ref[r], rows))


def row_source(refs, rows, e):
    north, main, south = refs
    if e < HALO:
        return north[e]
    if e < HALO + rows:
        return main[e - HALO]
    return south[e - HALO - rows]


def strip_kernel(*refs):
    seen, stat = refs[0:3], refs[3:6]
    east_ref, west_ref = refs[6:]
    rows, days, cols = seen[1].shape
    per = cols // HALO
    lane_seen = grid_of((days, cols), 1)
    lane_stat = grid_of((days + EXTRA, cols), 1)
    total = rows + 2 * HALO
    for tile in range(east_ref.shape[0]):
        for source, at, lane in (
            (seen, slice(0, days), lane_seen),
            (stat, slice(days, None), lane_stat),
        ):
            east = jnp.zeros(lane.shape, F32)
            west = jnp.zeros(lane.shape, F32)
            for j in range(min(per, total - tile * per)):
                value = row_source(source, rows, tile * per + j)
                here = (lane >= j * HALO) & (lane < (j + 1) * HALO)
                to_west = pltpu.roll(value, j * HALO, 1) if j else value
                to_east = pltpu.roll(value, (j + 1) * HALO, 1)
                west = jnp.where(here, to_west, west)
                east = jnp.where(here, to_east, east)
            east_ref[tile, at, :] = east
            west_ref[tile, at, :] = west


def project_rows(last, f_ref, out_ref, seen_ref, gap_ref, low, high):
    p0, p1 = halves(last)
    weights = jnp.concatenate([p0, p0, p1, p1], axis=1)

    def row(e, _):
        f0, f1 = halves(f_ref[e])
        stack = jnp.concatenate([f0, f1, f0, f1], axis=0)
        recon = jnp.dot(weights, stack, preferred_element_type=F32)
        out_ref[e] = seen_ref[e] + gap_ref[e] * recon
        return 0

    lax.fori_loop(low, high, row, 0, unroll=True)


def beside_matrix(width):
    row, col = grid_of((width, width), 0), grid_of((width, width), 1)
    apart = jnp.abs(row - col)
    near = jnp.where((apart == 1) | (apart == width - 1), 1.0, 0.0)
    return jnp.where(apart == 0, -4.0, near).astype(BF16)


def smooth_rows(near, f_ref, out_ref, gap_ref, diff_ref, low, high):
    total, days, width = f_ref.shape
    low = max(1, low - (low - high) % BATCH)
    steps = (high - low) // BATCH

    def batch(i, _):
        e = low + i * BATCH
        value = f_ref[pl.ds(e, BATCH)].reshape(BATCH * days, width)
        f0, f1 = halves(value)
        lap = jnp.dot(f0, near, preferred_element_type=F32) + jnp.dot(
            f1, near, preferred_element_type=F32
        )
        for k in range(BATCH):
            coef = jnp.broadcast_to(diff_ref[e + k], (CHUNK, width))
            for at in range(0, days, CHUNK):
                part = slice(at, at + CHUNK)
                around = f_ref[e + k - 1, part, :] + f_ref[e + k + 1, part, :]
                around = around + lap[k * days + at : k * days + at + CHUNK]
                out_ref[e + k, part, :] = (
                    f_ref[e + k, part, :] + (gap_ref[e + k, part, :] * coef) * around
                )
        return 0

    lax.fori_loop(0, steps, batch, 0, unroll=True)


def sweep_body(sweep, last, f_ref, a_ref, b_ref, seen_ref, gap_ref, diff_ref):
    total = seen_ref.shape[0]
    edge = sweep * PASSES
    project_rows(last, f_ref, a_ref, seen_ref, gap_ref, edge, total - edge)
    near = beside_matrix(seen_ref.shape[2])
    now, other = a_ref, b_ref
    for step in range(PASSES):
        edge += 1
        smooth_rows(near, now, other, gap_ref, diff_ref, edge, total - edge)
        now, other = other, now
    return now


def first_kernel(*refs):
    last_ref = refs[0]
    seen, stat = refs[1:4], refs[4:7]
    east_ref, west_ref = refs[7:9]
    seen_ref, gap_ref, diff_ref, out_ref, packed_ref = refs[9:14]
    a_ref = refs[14]
    rows, days, cols = seen[1].shape
    total = rows + 2 * HALO
    per = cols // HALO
    lane = grid_of((days, cols), 1)
    lane1 = grid_of((1, cols), 1)

    def side(e, at, lane):
        tile, j = e // per, e % per
        east, west = east_ref[tile, at, :], west_ref[tile, at, :]
        shift = (cols - j * HALO) % cols
        east = pltpu.roll(east, shift, 1) if shift else east
        west = pltpu.roll(west, cols - (j + 1) * HALO, 1)
        value = jnp.where(lane >= cols - HALO, west, 0.0)
        return jnp.where(lane < HALO, east, value)

    for e in range(total):
        seen_ref[e, :, :cols] = row_source(seen, rows, e)
        seen_ref[e, :, cols:] = side(e, slice(0, days), lane)
        whole = row_source(stat, rows, e)
        gap_ref[e, :, :cols] = whole[:days]
        gap_ref[e, :, cols:] = side(e, slice(days, 2 * days), lane)
        diff_ref[e, :, :cols] = whole[days : days + 1]
        diff_ref[e, :, cols:] = side(e, slice(2 * days, 2 * days + 1), lane1)
    now = sweep_body(
        0, last_ref[...], seen_ref, a_ref, out_ref, seen_ref, gap_ref, diff_ref
    )
    assert now is out_ref
    cov = covariance_of(lambda r: out_ref[HALO + r, :, :cols], rows)
    pack_symmetric(packed_ref, cov)


def next_kernel(sweep, last_ref, f_ref, seen_ref, gap_ref, diff_ref, out_ref, packed_ref, a_ref):
    now = sweep_body(sweep, last_ref[...], f_ref, a_ref, out_ref, seen_ref, gap_ref, diff_ref)
    assert now is out_ref
    rows = out_ref.shape[0] - 2 * HALO
    cols = out_ref.shape[2] // 2
    cov = covariance_of(lambda r: out_ref[HALO + r, :, :cols], rows)
    pack_symmetric(packed_ref, cov)


def end_kernel(sweep, last_ref, f_ref, seen_ref, gap_ref, diff_ref, rows_ref, out_ref, modes_ref, a_ref, b_ref):
    now = sweep_body(sweep, last_ref[...], f_ref, a_ref, b_ref, seen_ref, gap_ref, diff_ref)
    days, rows, cols = out_ref.shape
    flat = out_ref.reshape(days * rows, cols)
    for r in range(rows):
        flat[pl.ds(r, days, stride=rows), :] = now[HALO + r, :, :cols]
    modes_ref[...] = rows_ref[...].T


def call(kernel, name, ins, outs, scratch=(), scalars=0):
    specs = [SMEM] * scalars + [VMEM] * (len(ins) - scalars)
    return pl.pallas_call(
        kernel,
        name=name,
        out_shape=[jax.ShapeDtypeStruct(s, F32) for s in outs],
        in_specs=specs,
        out_specs=[VMEM] * len(outs),
        scratch_shapes=[pltpu.VMEM(s, F32) for s in scratch],
        compiler_params=pltpu.CompilerParams(vmem_limit_bytes=24 * 2**20),
    )(*ins)


def sum_parts(packed):
    count = lax.axis_size("band")
    width = packed.shape[2]
    parity = lax.rem(lax.axis_index("band"), 2)
    mine = lax.dynamic_slice_in_dim(packed, parity, 1, 0)
    other = lax.dynamic_slice_in_dim(packed, 1 - parity, 1, 0)
    got = lax.ppermute(other, "band", [(i, i ^ 1) for i in range(count)])
    everyone = count * lax.axis_size("wide")
    copies = jnp.broadcast_to(mine + got, (everyone, 1, width))
    return lax.all_to_all(copies, ("wide", "band"), 0, 0, tiled=True)


def edges(cells):
    rows = cells.shape[0]
    count = lax.axis_size("band")
    north = lax.ppermute(cells[rows - HALO :], "band", [(i, i + 1) for i in range(count - 1)])
    south = lax.ppermute(cells[:HALO], "band", [(i + 1, i) for i in range(count - 1)])
    return [north, cells, south]


def shards(day_field, obs_mask, ocean_mask, diffusivity, start_modes):
    days, rows, cols = obs_mask.shape
    modes = start_modes.shape[1]
    count = lax.axis_size("wide")
    me = lax.axis_index("wide")
    pieces, offs = [], []
    for k in range(count):
        to = lambda i: i ^ k
        piece = lax.dynamic_slice_in_dim(day_field, to(me) * cols, cols, 2)
        if k:
            piece = lax.ppermute(piece, "wide", [(i, to(i)) for i in range(count)])
        pieces.append(piece)
        offs.append(to(me) * day_field.shape[0])
    (stat,) = call(
        static_kernel, "static", [obs_mask, ocean_mask, diffusivity], [(rows, days + EXTRA, cols)]
    )
    stats = edges(stat)
    (basis,) = call(start_kernel, "start", [start_modes], [(modes, days)])
    offs = jnp.stack(offs).astype(jnp.int32)
    width = (days // 8 // 2 * 2 // 2 // 2 * 2 + 1) * LANES
    width = (days // 8 + 1) * LANES
    seen, packed = call(
        functools.partial(observed_kernel, count),
        "observed",
        [offs] + pieces + [stat],
        [(rows, days, cols), (2, 1, width)],
        scalars=1,
    )
    seens = edges(seen)
    parts = sum_parts(packed)
    total = rows + 2 * HALO
    tiles = pl.cdiv(total, cols // HALO)
    strip = (tiles, 2 * days + EXTRA, cols)
    east, west = call(strip_kernel, "strips", seens + stats, [strip, strip])
    from_west = lax.ppermute(east, "wide", [(i, (i + 1) % count) for i in range(count)])
    from_east = lax.ppermute(west, "wide", [((i + 1) % count, i) for i in range(count)])
    quarter = (days // 4, LANES)
    orth = lambda parts, basis: call(
        modes_kernel, "modes", [parts, basis], [(modes, days), (days, days)], [quarter]
    )
    wide_map, wide_row = (total, days, 2 * cols), (total, 1, 2 * cols)
    basis, last = orth(parts, basis)
    seen_w, gap_w, diff_w, filled, packed = call(
        first_kernel,
        "sweep0",
        [last] + seens + stats + [from_east, from_west],
        [wide_map, wide_map, wide_row, wide_map, (2, 1, width)],
        [wide_map],
    )
    for sweep in range(1, OUTER):
        basis, last = orth(sum_parts(packed), basis)
        ins = [last, filled, seen_w, gap_w, diff_w]
        if sweep < OUTER - 1:
            filled, packed = call(
                functools.partial(next_kernel, sweep),
                f"sweep{sweep}",
                ins,
                [wide_map, (2, 1, width)],
                [wide_map],
            )
        else:
            out, mode_basis = call(
                functools.partial(end_kernel, sweep),
                f"sweep{sweep}",
                ins + [basis],
                [(days, rows, cols), (days, modes)],
                [wide_map, wide_map],
            )
    return (out, mode_basis)


def solution(mesh):
    placed = (
        P("wide", "band", None),
        P(None, "band", "wide"),
        P("band", "wide"),
        P("band", "wide"),
        P(),
    )
    return jax.shard_map(
        shards,
        mesh=mesh,
        in_specs=placed,
        out_specs=(P(None, "band", "wide"), P()),
        check_vma=False,
    )
```

```python
import functools
import jax
import jax.numpy as jnp
from jax import lax
from jax.experimental import pallas as pl
from jax.experimental.pallas import tpu as pltpu
from jax.sharding import PartitionSpec as P

OUTER = 3
INNER = 3
PASSES = 3
HALO = OUTER * PASSES
LANES = 128
EXTRA = 8
CHUNK = 8
BATCH = 2
FLOOR = 0.1

F32 = jnp.float32
BF16 = jnp.bfloat16
VMEM = pl.BlockSpec(memory_space=pltpu.VMEM)
SMEM = pl.BlockSpec(memory_space=pltpu.SMEM)


def highest(left, right, left_dim, right_dim):
    return lax.dot_general(
        left,
        right,
        (((left_dim,), (right_dim,)), ((), ())),
        precision=lax.Precision.HIGHEST,
        preferred_element_type=F32,
    )


def halves(value):
    high = value.astype(BF16)
    return high, (value - high.astype(F32)).astype(BF16)


def thirds(value):
    first = value.astype(BF16)
    rest = value - first.astype(F32)
    second = rest.astype(BF16)
    return first, second, (rest - second.astype(F32)).astype(BF16)


def grid_of(shape, axis):
    return lax.broadcasted_iota(jnp.int32, shape, axis)


def covariance_of(rows_of, count):
    days = None
    total = None
    for start in range(0, count, 2):
        pair = jnp.concatenate([rows_of(start), rows_of(start + 1)], axis=1)
        days = pair.shape[0]
        stack = jnp.concatenate(thirds(pair), axis=0)
        part = lax.dot_general(
            stack, stack, (((1,), (1,)), ((), ())), preferred_element_type=F32
        )
        total = part if total is None else total + part
    block = lambda i, j: total[i * days : (i + 1) * days, j * days : (j + 1) * days]
    small = block(2, 2) + (block(1, 2) + block(2, 1))
    small = small + (block(0, 2) + block(2, 0)) + block(1, 1)
    return block(0, 0) + ((block(0, 1) + block(1, 0)) + small)


def pack_symmetric(packed_ref, cov):
    half = cov.shape[0] // 2
    quarter = half // 2
    upper = grid_of((half, half), 1) >= grid_of((half, half), 0)
    same = grid_of((half, half), 1) == grid_of((half, half), 0)
    low = cov[half:, half:]
    mixed = jnp.where(upper, cov[:half, :half], low)
    cross = cov[:half, half:]
    body = jnp.concatenate(
        [mixed[:quarter], cross[:quarter], mixed[quarter:], cross[quarter:]], axis=1
    )
    diagonal = jnp.sum(jnp.where(same, low, 0.0), axis=0, keepdims=True)
    diagonal = jnp.concatenate([diagonal, jnp.zeros((1, LANES - half), F32)], axis=1)
    each = quarter // 2
    for side in range(2):
        for row in range(each):
            packed_ref[side, :, row * LANES : (row + 1) * LANES] = body[
                side * each + row : side * each + row + 1
            ]
        packed_ref[side, :, each * LANES :] = (
            diagonal if side == 0 else jnp.zeros((1, LANES), F32)
        )


def unpack_symmetric(parts_ref, body_ref, days):
    half = days // 2
    quarter = half // 2
    each = quarter // 2
    sides = []
    for side in range(2):
        values = [parts_ref[j] for j in range(side, parts_ref.shape[0], 2)]
        while len(values) > 1:
            paired = [values[i] + values[i + 1] for i in range(0, len(values) - 1, 2)]
            values = paired + values[len(paired) * 2 :]
        sides.append(values[0])
        for row in range(each):
            body_ref[side * each + row : side * each + row + 1, :] = values[0][
                :, row * LANES : (row + 1) * LANES
            ]
    body = body_ref[...]
    diagonal = sides[0][:, each * LANES : each * LANES + half]
    mixed = jnp.concatenate([body[:, :half], body[:, 2 * half : 3 * half]], axis=0)
    cross = jnp.concatenate([body[:, half : 2 * half], body[:, 3 * half :]], axis=0)
    col, row = grid_of((half, half), 1), grid_of((half, half), 0)
    flipped = mixed.T
    high = jnp.where(col >= row, mixed, flipped)
    low = jnp.where(col < row, mixed, flipped)
    low = jnp.where(col == row, jnp.broadcast_to(diagonal, (half, half)), low)
    top = jnp.concatenate([high, cross], axis=1)
    bottom = jnp.concatenate([cross.T, low], axis=1)
    return jnp.concatenate([top, bottom], axis=0)


def spread(value, at):
    return jnp.broadcast_to(value[at : at + 1], value.shape)


def column_spread(value, at, zero):
    return jnp.broadcast_to(value[:, at : at + 1], value.shape) + zero


def block_pivots(lead, own, zero):
    sublane = grid_of(lead.shape, 0)
    below, solved = lead, lead
    columns = [column_spread(lead, own + m, zero) for m in range(8)]
    pivots = jnp.ones(lead.shape, F32)
    for k in range(0, 8, 2):
        left, right = columns[k], columns[k + 1]
        a, b, c = spread(left, k), spread(left, k + 1), spread(right, k + 1)
        scale = 1.0 / (a * c - b * b)
        ratio = b * (1.0 / a)
        first, second = sublane == k, sublane == k + 1
        g0 = (left * c - right * b) * scale
        g1 = (right * a - left * b) * scale
        h0 = jnp.where(first, 1.0 - c * scale, jnp.where(second, b * scale, g0))
        h1 = jnp.where(first, b * scale, jnp.where(second, 1.0 - a * scale, g1))
        for m in range(k + 2, 8):
            top, low = spread(columns[m], k), spread(columns[m], k + 1)
            columns[m] = columns[m] - (h0 * top + h1 * low)
        solved = solved - (h0 * spread(solved, k) + h1 * spread(solved, k + 1))
        f0 = jnp.where(sublane > k + 1, g0, jnp.where(second, ratio, 0.0))
        f1 = jnp.where(sublane > k + 1, g1, 0.0)
        below = below - (f0 * spread(below, k) + f1 * spread(below, k + 1))
        pivots = jnp.where(first, a, jnp.where(second, c - b * ratio, pivots))
    return below, solved, pivots


def orthonormal_rows(rows):
    count, width = rows.shape
    gram = highest(rows, rows, 1, 1)
    pad = jnp.zeros((count, LANES - count - width), F32)
    table = jnp.concatenate([gram, rows, pad], axis=1)
    groups = [table[8 * i : 8 * i + 8] for i in range(count // 8)]
    lane, sublane = grid_of((8, LANES), 1), grid_of((8, LANES), 0)
    zero = jnp.where(lane < 0, 1.0, 0.0)
    outs, worst = [], None
    for i, lead in enumerate(groups):
        below, solved, pivots = block_pivots(lead, 8 * i, zero)
        factors = [spread(solved, m) for m in range(8)]
        for j in range(i + 1, len(groups)):
            terms = [
                column_spread(groups[j], 8 * i + m, zero) * factors[m] for m in range(8)
            ]
            while len(terms) > 1:
                terms = [terms[n] + terms[n + 1] for n in range(0, len(terms), 2)]
            groups[j] = groups[j] - terms[0]
        start = jnp.where(lane == sublane + 8 * i, table[8 * i : 8 * i + 8], 0.0)
        kept = pivots / jnp.sum(start, axis=1, keepdims=True)
        worst = kept if worst is None else jnp.minimum(worst, kept)
        outs.append(below[:, count : count + width] * lax.rsqrt(pivots)[:, :width])
    return jnp.concatenate(outs, axis=0), jnp.min(worst)


def careful_rows(rows):
    count, width = rows.shape
    gram = highest(rows, rows, 1, 1)
    pad = jnp.zeros((count, LANES - count - width), F32)
    table = jnp.concatenate([gram, rows, pad], axis=1)
    groups = [table[8 * i : 8 * i + 8] for i in range(count // 8)]
    sublane = grid_of((8, LANES), 0)
    pivots = []
    repeat = lambda row: jnp.broadcast_to(row, (8, LANES))
    for k in range(0, count, 2):
        i, s = k // 8, k % 8
        first = [jnp.broadcast_to(g[:, k : k + 1], (8, LANES)) for g in groups[i:]]
        second = [jnp.broadcast_to(g[:, k + 1 : k + 2], (8, LANES)) for g in groups[i:]]
        row0, row1 = repeat(groups[i][s : s + 1]), repeat(groups[i][s + 1 : s + 2])
        a = repeat(first[0][s : s + 1])
        b = repeat(first[0][s + 1 : s + 2])
        c = repeat(second[0][s + 1 : s + 2])
        det = a * c - b * b
        scale = 1.0 / det
        h0, h1, h2 = c * scale, b * scale, a * scale
        w0 = h0 * row0 - h1 * row1
        w1 = h2 * row1 - h1 * row0
        ratio = b / a
        pivots.append((a, c - b * ratio))
        for j in range(i, len(groups)):
            c0, c1 = first[j - i], second[j - i]
            updated = groups[j] - (c0 * w0 + c1 * w1)
            if j == i:
                updated = jnp.where(sublane > s + 1, updated, groups[j])
                updated = jnp.where(sublane == s + 1, row1 - ratio * row0, updated)
            groups[j] = updated
    outs = []
    for i, g in enumerate(groups):
        d = jnp.zeros((8, LANES), F32)
        for s in range(8):
            d = jnp.where(sublane == s, pivots[(8 * i + s) // 2][s % 2], d)
        outs.append(g[:, count : count + width] * lax.rsqrt(d)[:, :width])
    return jnp.concatenate(outs, axis=0)


def start_kernel(modes_ref, rows_ref):
    modes = modes_ref[...]
    rows_ref[...], kept = orthonormal_rows(modes)

    @pl.when(jnp.logical_not(kept >= FLOOR))
    def _():
        rows_ref[...] = careful_rows(modes)


def modes_kernel(parts_ref, rows_ref, new_ref, last_ref, body_ref):
    rows = rows_ref[...]
    days = rows.shape[1]
    cov = unpack_symmetric(parts_ref, body_ref, days)
    same = grid_of((days, days), 1) == grid_of((days, days), 0)
    peak = jnp.max(jnp.where(same, cov, 0.0), keepdims=True)
    cov = cov * (1.0 / peak)
    moved = highest(rows, cov, 1, 0)
    twice = highest(cov, cov, 1, 0)
    new, kept = orthonormal_rows(highest(moved, twice, 1, 0))
    new_ref[...] = new
    last_ref[...] = highest(new, new, 0, 0)

    @pl.when(jnp.logical_not(kept >= FLOOR))
    def _():
        def step(_, held):
            return careful_rows(highest(held, cov, 1, 0))

        again = lax.fori_loop(0, INNER, step, rows)
        new_ref[...] = again
        last_ref[...] = highest(again, again, 0, 0)


def static_kernel(obs_ref, ocean_ref, diff_ref, stat_ref):
    days, rows, cols = obs_ref.shape
    flat = obs_ref.reshape(days * rows, cols)
    for r in range(rows):
        seen = flat[pl.ds(r, days, stride=rows), :]
        ocean = ocean_ref[r : r + 1, :]
        stat_ref[r, :days, :] = ((1 - seen) * ocean).astype(F32)
        rest = jnp.concatenate(
            [
                diff_ref[r : r + 1, :],
                ocean.astype(F32),
                jnp.zeros((EXTRA - 2, cols), F32),
            ],
            axis=0,
        )
        stat_ref[r, days:, :] = rest


def observed_kernel(blocks, offs_ref, *refs):
    piece_refs = refs[:blocks]
    stat_ref, _, seen_ref, head_ref, tail_ref, packed_ref = refs[blocks:]
    rows, days, cols = seen_ref.shape
    each = piece_refs[0].shape[0]
    for r in range(rows):
        ocean = stat_ref[r, days + 1 : days + 2, :]
        for b, piece_ref in enumerate(piece_refs):
            flat = piece_ref.reshape(each * rows, cols)
            start = pl.multiple_of(offs_ref[b], each)
            gap = stat_ref[r, pl.ds(start, each), :]
            value = flat[pl.ds(r, each, stride=rows), :]
            seen_ref[r, pl.ds(start, each), :] = value * (ocean - gap)
    for r in range(HALO):
        head_ref[r] = seen_ref[r]
        tail_ref[r] = seen_ref[rows - HALO + r]
    pack_symmetric(packed_ref, covariance_of(lambda r: seen_ref[r], rows))


def row_source(refs, rows, e):
    north, main, south = refs
    if e < HALO:
        return north[e]
    if e < HALO + rows:
        return main[e - HALO]
    return south[e - HALO - rows]


def strip_rows(sweep, total):
    return range(sweep * PASSES + 1, total - sweep * PASSES - 1)


def strip_place(sweep, e, cols):
    per = cols // (2 * PASSES)
    at = e - sweep * PASSES - 1
    return at // per, at % per * 2 * PASSES


def write_strips(sweep, total, value_of, strip_ref, at):
    _, _, cols = strip_ref.shape
    tiles = {}
    for e in strip_rows(sweep, total):
        value = value_of(e)
        tile, place = strip_place(sweep, e, cols)
        lane = grid_of(value.shape, 1)
        here = (lane >= place) & (lane < place + 2 * PASSES)
        moved = pltpu.roll(value, place + PASSES, 1)
        tiles[tile] = jnp.where(here, moved, tiles.get(tile, 0.0))
    for tile, value in tiles.items():
        strip_ref[tile, at, :] = value


def read_strips(sweep, total, west_ref, east_ref, at):
    _, _, cols = west_ref.shape
    merged = []
    for tile in range(west_ref.shape[0]):
        west, east = west_ref[tile, at, :], east_ref[tile, at, :]
        lane = grid_of(west.shape, 1)
        merged.append(jnp.where(lane % (2 * PASSES) < PASSES, west, east))

    def side(e):
        lane = grid_of(merged[0].shape, 1)
        if e not in strip_rows(sweep, total):
            return jnp.zeros(merged[0].shape, F32)
        tile, place = strip_place(sweep, e, cols)
        moved = pltpu.roll(merged[tile], cols - place - PASSES, 1)
        return jnp.where((lane < PASSES) | (lane >= cols - PASSES), moved, 0.0)

    return side


def first_strip_kernel(*refs):
    seen, stat, strip_ref = refs[0:3], refs[3:6], refs[6]
    rows, days, _ = seen[1].shape
    total = rows + 2 * HALO
    write_strips(0, total, lambda e: row_source(seen, rows, e), strip_ref, slice(0, days))
    write_strips(0, total, lambda e: row_source(stat, rows, e), strip_ref, slice(days, None))


def strip_kernel(sweep, f_ref, strip_ref):
    cols = strip_ref.shape[2]
    total = f_ref.shape[0]
    write_strips(sweep, total, lambda e: f_ref[e, :, :cols], strip_ref, slice(None))


def project_rows(last, row_of, out_ref, seen_ref, gap_ref, low, high):
    p0, p1 = halves(last)
    weights = jnp.concatenate([p0, p0, p1, p1], axis=1)

    for e in range(low, high):
        f0, f1 = halves(row_of(e))
        stack = jnp.concatenate([f0, f1, f0, f1], axis=0)
        recon = jnp.dot(weights, stack, preferred_element_type=F32)
        out_ref[e] = seen_ref[e] + gap_ref[e] * recon


def beside_matrix(width):
    row, col = grid_of((width, width), 0), grid_of((width, width), 1)
    apart = jnp.abs(row - col)
    near = jnp.where((apart == 1) | (apart == width - 1), 1.0, 0.0)
    return jnp.where(apart == 0, -4.0, near).astype(BF16)


def smooth_rows(near, f_ref, out_ref, gap_ref, diff_ref, low, high):
    _, days, width = f_ref.shape
    for e in range(low, high, BATCH):
        value = f_ref[e : e + BATCH].reshape(BATCH * days, width)
        f0, f1 = halves(value)
        lap = jnp.dot(f0, near, preferred_element_type=F32)
        lap = lap + jnp.dot(f1, near, preferred_element_type=F32)
        for k in range(BATCH):
            coef = jnp.broadcast_to(diff_ref[e + k], (CHUNK, width))
            for at in range(0, days, CHUNK):
                part = slice(at, at + CHUNK)
                around = f_ref[e + k - 1, part, :] + f_ref[e + k + 1, part, :]
                around = around + lap[k * days + at : k * days + at + CHUNK]
                out_ref[e + k, part, :] = (
                    f_ref[e + k, part, :] + (gap_ref[e + k, part, :] * coef) * around
                )


def sweep_body(sweep, last, row_of, a_ref, b_ref, seen_ref, gap_ref, diff_ref):
    total = seen_ref.shape[0]
    edge = sweep * PASSES
    project_rows(last, row_of, a_ref, seen_ref, gap_ref, edge, total - edge)
    near = beside_matrix(seen_ref.shape[2])
    now, other = a_ref, b_ref
    for step in range(PASSES):
        edge += 1
        smooth_rows(near, now, other, gap_ref, diff_ref, edge, total - edge)
        now, other = other, now
    return now


def joined(f_ref, side, cols):
    return lambda e: jnp.concatenate([f_ref[e, :, :cols], side(e)], axis=1)


def first_kernel(*refs):
    last_ref = refs[0]
    seen, stat = refs[1:4], refs[4:7]
    west_ref, east_ref = refs[7:9]
    seen_ref, gap_ref, diff_ref, out_ref, packed_ref, a_ref = refs[9:]
    rows, days, cols = seen[1].shape
    total = rows + 2 * HALO
    seen_side = read_strips(0, total, west_ref, east_ref, slice(0, days))
    stat_side = read_strips(0, total, west_ref, east_ref, slice(days, None))
    for e in range(total):
        seen_ref[e, :, :cols] = row_source(seen, rows, e)
        seen_ref[e, :, cols:] = seen_side(e)
        main, side = row_source(stat, rows, e), stat_side(e)
        gap_ref[e, :, :cols] = main[:days]
        gap_ref[e, :, cols:] = side[:days]
        diff_ref[e, :, :cols] = main[days : days + 1]
        diff_ref[e, :, cols:] = side[days : days + 1]
    row_of = lambda e: seen_ref[e]
    now = sweep_body(0, last_ref[...], row_of, a_ref, out_ref, seen_ref, gap_ref, diff_ref)
    assert now is out_ref
    cov = covariance_of(lambda r: out_ref[HALO + r, :, :cols], rows)
    pack_symmetric(packed_ref, cov)


def next_kernel(sweep, *refs):
    last_ref, f_ref, west_ref, east_ref, seen_ref, gap_ref, diff_ref = refs[:7]
    out_ref, packed_ref, a_ref = refs[7:]
    total, cols = seen_ref.shape[0], west_ref.shape[2]
    side = read_strips(sweep, total, west_ref, east_ref, slice(None))
    row_of = joined(f_ref, side, cols)
    now = sweep_body(sweep, last_ref[...], row_of, a_ref, out_ref, seen_ref, gap_ref, diff_ref)
    assert now is out_ref
    cov = covariance_of(lambda r: out_ref[HALO + r, :, :cols], total - 2 * HALO)
    pack_symmetric(packed_ref, cov)


def end_kernel(sweep, *refs):
    last_ref, f_ref, west_ref, east_ref, seen_ref, gap_ref, diff_ref = refs[:7]
    out_ref, a_ref, b_ref = refs[7:]
    days, rows, cols = out_ref.shape
    side = read_strips(sweep, seen_ref.shape[0], west_ref, east_ref, slice(None))
    row_of = joined(f_ref, side, cols)
    now = sweep_body(sweep, last_ref[...], row_of, a_ref, b_ref, seen_ref, gap_ref, diff_ref)
    flat = out_ref.reshape(days * rows, cols)
    for r in range(rows):
        flat[pl.ds(r, days, stride=rows), :] = now[HALO + r, :, :cols]


def call(kernel, name, ins, outs, scratch=(), scalars=0):
    specs = [SMEM] * scalars + [VMEM] * (len(ins) - scalars)
    return pl.pallas_call(
        kernel,
        name=name,
        out_shape=[jax.ShapeDtypeStruct(s, F32) for s in outs],
        in_specs=specs,
        out_specs=[VMEM] * len(outs),
        scratch_shapes=[pltpu.VMEM(s, F32) for s in scratch],
        compiler_params=pltpu.CompilerParams(vmem_limit_bytes=24 * 2**20),
    )(*ins)


def pair_sums(packed):
    count = lax.axis_size("band")
    width = packed.shape[2]
    parity = lax.rem(lax.axis_index("band"), 2)
    mine = lax.dynamic_slice_in_dim(packed, parity, 1, 0)
    other = lax.dynamic_slice_in_dim(packed, 1 - parity, 1, 0)
    got = lax.ppermute(other, "band", [(i, i ^ 1) for i in range(count)])
    everyone = count * lax.axis_size("wide")
    return jnp.broadcast_to(mine + got, (everyone, 1, width))


def trade(copies):
    return lax.all_to_all(copies, ("wide", "band"), 0, 0, tiled=True)


def edges(head, cells, tail):
    count = lax.axis_size("band")
    north = lax.ppermute(tail, "band", [(i, i + 1) for i in range(count - 1)])
    south = lax.ppermute(head, "band", [(i + 1, i) for i in range(count - 1)])
    return [north, cells, south]


def beside(strip):
    count = lax.axis_size("wide")
    from_west = lax.ppermute(strip, "wide", [(i, (i + 1) % count) for i in range(count)])
    from_east = lax.ppermute(strip, "wide", [((i + 1) % count, i) for i in range(count)])
    return [from_west, from_east]


def shards(day_field, obs_mask, ocean_mask, diffusivity, start_modes):
    days, rows, cols = obs_mask.shape
    modes = start_modes.shape[1]
    count = lax.axis_size("wide")
    me = lax.axis_index("wide")
    pieces, offs = [], []
    for k in range(count):
        to = lambda i: i ^ k
        piece = lax.dynamic_slice_in_dim(day_field, to(me) * cols, cols, 2)
        if k:
            piece = lax.ppermute(piece, "wide", [(i, to(i)) for i in range(count)])
        pieces.append(piece)
        offs.append(to(me) * day_field.shape[0])
    offs = jnp.stack(offs).astype(jnp.int32)
    (stat,) = call(
        static_kernel, "static", [obs_mask, ocean_mask, diffusivity], [(rows, days + EXTRA, cols)]
    )
    stats = edges(stat[:HALO], stat, stat[rows - HALO :])
    (basis,) = call(start_kernel, "start", [start_modes.T], [(modes, days)])
    width = (days // 8 + 1) * LANES
    row_strip = (HALO, days, cols)
    seen, head, tail, packed = call(
        functools.partial(observed_kernel, count),
        "observed",
        [offs] + pieces + [stat, basis],
        [(rows, days, cols), row_strip, row_strip, (2, 1, width)],
        scalars=1,
    )
    seens = edges(head, seen, tail)
    total = rows + 2 * HALO
    strip_shape = lambda sweep, depth: (
        pl.cdiv(len(strip_rows(sweep, total)), cols // (2 * PASSES)),
        depth,
        cols,
    )
    wide_map, wide_row = (total, days, 2 * cols), (total, 1, 2 * cols)
    parts = trade(pair_sums(packed))
    (strip,) = call(
        first_strip_kernel, "strips0", seens + stats, [strip_shape(0, 2 * days + EXTRA)]
    )
    sides = beside(strip)
    for sweep in range(OUTER):
        basis, last = call(
            modes_kernel,
            "modes",
            [parts, basis],
            [(modes, days), (days, days)],
            [(days // 4, LANES)],
        )
        if sweep == 0:
            seen_w, gap_w, diff_w, filled, packed = call(
                first_kernel,
                "sweep0",
                [last] + seens + stats + sides,
                [wide_map, wide_map, wide_row, wide_map, (2, 1, width)],
                [wide_map],
            )
        elif sweep < OUTER - 1:
            filled, packed = call(
                functools.partial(next_kernel, sweep),
                f"sweep{sweep}",
                [last, filled] + sides + [seen_w, gap_w, diff_w],
                [wide_map, (2, 1, width)],
                [wide_map],
            )
        else:
            (out,) = call(
                functools.partial(end_kernel, sweep),
                f"sweep{sweep}",
                [last, filled] + sides + [seen_w, gap_w, diff_w],
                [(days, rows, cols)],
                [wide_map, wide_map],
            )
            return (out, basis.T)
        copies, held = lax.optimization_barrier((pair_sums(packed), filled))
        parts = trade(copies)
        (strip,) = call(
            functools.partial(strip_kernel, sweep + 1),
            f"strips{sweep + 1}",
            [held],
            [strip_shape(sweep + 1, days)],
        )
        sides = beside(strip)


def solution(mesh):
    placed = (
        P("wide", "band", None),
        P(None, "band", "wide"),
        P("band", "wide"),
        P("band", "wide"),
        P(),
    )
    return jax.shard_map(
        shards,
        mesh=mesh,
        in_specs=placed,
        out_specs=(P(None, "band", "wide"), P()),
        check_vma=False,
    )
```

```python
import functools
import jax
import jax.numpy as jnp
from jax import lax
from jax.experimental import pallas as pl
from jax.experimental.pallas import tpu as pltpu
from jax.sharding import PartitionSpec as P

OUTER = 3
INNER = 3
PASSES = 3
HALO = OUTER * PASSES
LANES = 128
EXTRA = 8
CHUNK = 8
BATCH = 2
FLOOR = 0.1

F32 = jnp.float32
BF16 = jnp.bfloat16
VMEM = pl.BlockSpec(memory_space=pltpu.VMEM)
SMEM = pl.BlockSpec(memory_space=pltpu.SMEM)


def highest(left, right, left_dim, right_dim):
    return lax.dot_general(
        left,
        right,
        (((left_dim,), (right_dim,)), ((), ())),
        precision=lax.Precision.HIGHEST,
        preferred_element_type=F32,
    )


def halves(value):
    high = value.astype(BF16)
    return high, (value - high.astype(F32)).astype(BF16)


def thirds(value):
    first = value.astype(BF16)
    rest = value - first.astype(F32)
    second = rest.astype(BF16)
    return first, second, (rest - second.astype(F32)).astype(BF16)


def grid_of(shape, axis):
    return lax.broadcasted_iota(jnp.int32, shape, axis)


def covariance_of(rows_of, count):
    days = None
    total = None
    for start in range(0, count, 2):
        pair = jnp.concatenate([rows_of(start), rows_of(start + 1)], axis=1)
        days = pair.shape[0]
        stack = jnp.concatenate(thirds(pair), axis=0)
        part = lax.dot_general(
            stack, stack, (((1,), (1,)), ((), ())), preferred_element_type=F32
        )
        total = part if total is None else total + part
    block = lambda i, j: total[i * days : (i + 1) * days, j * days : (j + 1) * days]
    small = block(2, 2) + (block(1, 2) + block(2, 1))
    small = small + (block(0, 2) + block(2, 0)) + block(1, 1)
    return block(0, 0) + ((block(0, 1) + block(1, 0)) + small)


def pack_symmetric(packed_ref, cov):
    half = cov.shape[0] // 2
    quarter = half // 2
    upper = grid_of((half, half), 1) >= grid_of((half, half), 0)
    same = grid_of((half, half), 1) == grid_of((half, half), 0)
    low = cov[half:, half:]
    mixed = jnp.where(upper, cov[:half, :half], low)
    cross = cov[:half, half:]
    body = jnp.concatenate(
        [mixed[:quarter], cross[:quarter], mixed[quarter:], cross[quarter:]], axis=1
    )
    diagonal = jnp.sum(jnp.where(same, low, 0.0), axis=0, keepdims=True)
    diagonal = jnp.concatenate([diagonal, jnp.zeros((1, LANES - half), F32)], axis=1)
    each = quarter // 2
    for side in range(2):
        for row in range(each):
            packed_ref[side, :, row * LANES : (row + 1) * LANES] = body[
                side * each + row : side * each + row + 1
            ]
        packed_ref[side, :, each * LANES :] = (
            diagonal if side == 0 else jnp.zeros((1, LANES), F32)
        )


def unpack_symmetric(parts_ref, body_ref, days):
    half = days // 2
    quarter = half // 2
    each = quarter // 2
    sides = []
    for side in range(2):
        values = [parts_ref[j] for j in range(side, parts_ref.shape[0], 2)]
        while len(values) > 1:
            paired = [values[i] + values[i + 1] for i in range(0, len(values) - 1, 2)]
            values = paired + values[len(paired) * 2 :]
        sides.append(values[0])
        for row in range(each):
            body_ref[side * each + row : side * each + row + 1, :] = values[0][
                :, row * LANES : (row + 1) * LANES
            ]
    body = body_ref[...]
    diagonal = sides[0][:, each * LANES : each * LANES + half]
    mixed = jnp.concatenate([body[:, :half], body[:, 2 * half : 3 * half]], axis=0)
    cross = jnp.concatenate([body[:, half : 2 * half], body[:, 3 * half :]], axis=0)
    col, row = grid_of((half, half), 1), grid_of((half, half), 0)
    flipped = mixed.T
    high = jnp.where(col >= row, mixed, flipped)
    low = jnp.where(col < row, mixed, flipped)
    low = jnp.where(col == row, jnp.broadcast_to(diagonal, (half, half)), low)
    top = jnp.concatenate([high, cross], axis=1)
    bottom = jnp.concatenate([cross.T, low], axis=1)
    return jnp.concatenate([top, bottom], axis=0)


def spread(value, at):
    return jnp.broadcast_to(value[at : at + 1], value.shape)


def column_spread(value, at, zero):
    return jnp.broadcast_to(value[:, at : at + 1], value.shape) + zero


def block_pivots(lead, own, zero):
    sublane = grid_of(lead.shape, 0)
    below, solved = lead, lead
    columns = [column_spread(lead, own + m, zero) for m in range(8)]
    pivots = jnp.ones(lead.shape, F32)
    for k in range(0, 8, 2):
        left, right = columns[k], columns[k + 1]
        a, b, c = spread(left, k), spread(left, k + 1), spread(right, k + 1)
        scale = 1.0 / (a * c - b * b)
        ratio = b * (1.0 / a)
        first, second = sublane == k, sublane == k + 1
        g0 = (left * c - right * b) * scale
        g1 = (right * a - left * b) * scale
        h0 = jnp.where(first, 1.0 - c * scale, jnp.where(second, b * scale, g0))
        h1 = jnp.where(first, b * scale, jnp.where(second, 1.0 - a * scale, g1))
        for m in range(k + 2, 8):
            top, low = spread(columns[m], k), spread(columns[m], k + 1)
            columns[m] = columns[m] - (h0 * top + h1 * low)
        solved = solved - (h0 * spread(solved, k) + h1 * spread(solved, k + 1))
        f0 = jnp.where(sublane > k + 1, g0, jnp.where(second, ratio, 0.0))
        f1 = jnp.where(sublane > k + 1, g1, 0.0)
        below = below - (f0 * spread(below, k) + f1 * spread(below, k + 1))
        pivots = jnp.where(first, a, jnp.where(second, c - b * ratio, pivots))
    return below, solved, pivots


def orthonormal_rows(rows):
    count, width = rows.shape
    gram = highest(rows, rows, 1, 1)
    pad = jnp.zeros((count, LANES - count - width), F32)
    table = jnp.concatenate([gram, rows, pad], axis=1)
    groups = [table[8 * i : 8 * i + 8] for i in range(count // 8)]
    lane, sublane = grid_of((8, LANES), 1), grid_of((8, LANES), 0)
    zero = jnp.where(lane < 0, 1.0, 0.0)
    outs, worst = [], None
    for i, lead in enumerate(groups):
        below, solved, pivots = block_pivots(lead, 8 * i, zero)
        factors = [spread(solved, m) for m in range(8)]
        for j in range(i + 1, len(groups)):
            terms = [
                column_spread(groups[j], 8 * i + m, zero) * factors[m] for m in range(8)
            ]
            while len(terms) > 1:
                terms = [terms[n] + terms[n + 1] for n in range(0, len(terms), 2)]
            groups[j] = groups[j] - terms[0]
        start = jnp.where(lane == sublane + 8 * i, table[8 * i : 8 * i + 8], 0.0)
        kept = pivots / jnp.sum(start, axis=1, keepdims=True)
        worst = kept if worst is None else jnp.minimum(worst, kept)
        outs.append(below[:, count : count + width] * lax.rsqrt(pivots)[:, :width])
    return jnp.concatenate(outs, axis=0), jnp.min(worst)


def careful_rows(rows):
    count, width = rows.shape
    gram = highest(rows, rows, 1, 1)
    pad = jnp.zeros((count, LANES - count - width), F32)
    table = jnp.concatenate([gram, rows, pad], axis=1)
    groups = [table[8 * i : 8 * i + 8] for i in range(count // 8)]
    sublane = grid_of((8, LANES), 0)
    pivots = []
    repeat = lambda row: jnp.broadcast_to(row, (8, LANES))
    for k in range(0, count, 2):
        i, s = k // 8, k % 8
        first = [jnp.broadcast_to(g[:, k : k + 1], (8, LANES)) for g in groups[i:]]
        second = [jnp.broadcast_to(g[:, k + 1 : k + 2], (8, LANES)) for g in groups[i:]]
        row0, row1 = repeat(groups[i][s : s + 1]), repeat(groups[i][s + 1 : s + 2])
        a = repeat(first[0][s : s + 1])
        b = repeat(first[0][s + 1 : s + 2])
        c = repeat(second[0][s + 1 : s + 2])
        det = a * c - b * b
        scale = 1.0 / det
        h0, h1, h2 = c * scale, b * scale, a * scale
        w0 = h0 * row0 - h1 * row1
        w1 = h2 * row1 - h1 * row0
        ratio = b / a
        pivots.append((a, c - b * ratio))
        for j in range(i, len(groups)):
            c0, c1 = first[j - i], second[j - i]
            updated = groups[j] - (c0 * w0 + c1 * w1)
            if j == i:
                updated = jnp.where(sublane > s + 1, updated, groups[j])
                updated = jnp.where(sublane == s + 1, row1 - ratio * row0, updated)
            groups[j] = updated
    outs = []
    for i, g in enumerate(groups):
        d = jnp.zeros((8, LANES), F32)
        for s in range(8):
            d = jnp.where(sublane == s, pivots[(8 * i + s) // 2][s % 2], d)
        outs.append(g[:, count : count + width] * lax.rsqrt(d)[:, :width])
    return jnp.concatenate(outs, axis=0)


def start_kernel(modes_ref, rows_ref):
    modes = modes_ref[...]
    rows_ref[...], kept = orthonormal_rows(modes)

    @pl.when(jnp.logical_not(kept >= FLOOR))
    def _():
        rows_ref[...] = careful_rows(modes)


def modes_kernel(parts_ref, rows_ref, new_ref, last_ref, body_ref):
    rows = rows_ref[...]
    days = rows.shape[1]
    cov = unpack_symmetric(parts_ref, body_ref, days)
    same = grid_of((days, days), 1) == grid_of((days, days), 0)
    peak = jnp.max(jnp.where(same, cov, 0.0), keepdims=True)
    cov = cov * (1.0 / peak)
    moved = highest(rows, cov, 1, 0)
    twice = highest(cov, cov, 1, 0)
    new, kept = orthonormal_rows(highest(moved, twice, 1, 0))
    new_ref[...] = new
    last_ref[...] = highest(new, new, 0, 0)

    @pl.when(jnp.logical_not(kept >= FLOOR))
    def _():
        def step(_, held):
            return careful_rows(highest(held, cov, 1, 0))

        again = lax.fori_loop(0, INNER, step, rows)
        new_ref[...] = again
        last_ref[...] = highest(again, again, 0, 0)


def static_kernel(obs_ref, ocean_ref, diff_ref, stat_ref):
    days, rows, cols = obs_ref.shape
    flat = obs_ref.reshape(days * rows, cols)
    for r in range(rows):
        seen = flat[pl.ds(r, days, stride=rows), :]
        ocean = ocean_ref[r : r + 1, :]
        stat_ref[r, :days, :] = ((1 - seen) * ocean).astype(F32)
        rest = jnp.concatenate(
            [
                diff_ref[r : r + 1, :],
                ocean.astype(F32),
                jnp.zeros((EXTRA - 2, cols), F32),
            ],
            axis=0,
        )
        stat_ref[r, days:, :] = rest


def observed_kernel(blocks, offs_ref, *refs):
    piece_refs = refs[:blocks]
    stat_ref, _, seen_ref, head_ref, tail_ref, packed_ref = refs[blocks:]
    rows, days, cols = seen_ref.shape
    each = piece_refs[0].shape[0]
    for r in range(rows):
        ocean = stat_ref[r, days + 1 : days + 2, :]
        for b, piece_ref in enumerate(piece_refs):
            flat = piece_ref.reshape(each * rows, cols)
            start = pl.multiple_of(offs_ref[b], each)
            gap = stat_ref[r, pl.ds(start, each), :]
            value = flat[pl.ds(r, each, stride=rows), :]
            seen_ref[r, pl.ds(start, each), :] = value * (ocean - gap)
    for r in range(HALO):
        head_ref[r] = seen_ref[r]
        tail_ref[r] = seen_ref[rows - HALO + r]
    pack_symmetric(packed_ref, covariance_of(lambda r: seen_ref[r], rows))


def row_source(refs, rows, e):
    north, main, south = refs
    if e < HALO:
        return north[e]
    if e < HALO + rows:
        return main[e - HALO]
    return south[e - HALO - rows]


def strip_places(rows, cols):
    reach = {}
    for e in range(rows + 2 * HALO):
        reach[e] = HALO - max(0, HALO - e, e - HALO - rows + 1)
    places, tile, at = {}, 0, 0
    for e in sorted(reach, key=lambda e: (-reach[e], e)):
        if not reach[e]:
            continue
        if at + reach[e] > cols:
            tile, at = tile + 1, 0
        places[e] = (tile, at, reach[e])
        at += reach[e]
    return places, tile + 1


def strip_kernel(*refs):
    seen, stat = refs[0:3], refs[3:6]
    east_ref, west_ref = refs[6:]
    rows, days, cols = seen[1].shape
    places, tiles = strip_places(rows, cols)
    for source, at in ((seen, slice(0, days)), (stat, slice(days, None))):
        for tile in range(tiles):
            east = west = 0.0
            for e, (where, place, reach) in places.items():
                if where != tile:
                    continue
                value = row_source(source, rows, e)
                lane = grid_of(value.shape, 1)
                here = (lane >= place) & (lane < place + reach)
                to_west = pltpu.roll(value, place, 1) if place else value
                west = jnp.where(here, to_west, west)
                east = jnp.where(here, pltpu.roll(value, place + reach, 1), east)
            east_ref[tile, at, :] = east
            west_ref[tile, at, :] = west


def strip_side(rows, west_ref, east_ref, at, e):
    _, _, cols = west_ref.shape
    places, _ = strip_places(rows, cols)
    if e not in places:
        return jnp.zeros(west_ref[0, at, :].shape, F32)
    tile, place, reach = places[e]
    west, east = west_ref[tile, at, :], east_ref[tile, at, :]
    lane = grid_of(west.shape, 1)
    east = pltpu.roll(east, cols - place, 1) if place else east
    west = pltpu.roll(west, cols - reach - place, 1)
    value = jnp.where(lane >= cols - reach, west, 0.0)
    return jnp.where(lane < reach, east, value)


def project_rows(last, row_of, out_ref, seen_ref, gap_ref, low, high):
    p0, p1 = halves(last)
    weights = jnp.concatenate([p0, p0, p1, p1], axis=1)

    for e in range(low, high):
        f0, f1 = halves(row_of(e))
        stack = jnp.concatenate([f0, f1, f0, f1], axis=0)
        recon = jnp.dot(weights, stack, preferred_element_type=F32)
        out_ref[e] = seen_ref[e] + gap_ref[e] * recon


def beside_matrix(width):
    row, col = grid_of((width, width), 0), grid_of((width, width), 1)
    apart = jnp.abs(row - col)
    near = jnp.where((apart == 1) | (apart == width - 1), 1.0, 0.0)
    return jnp.where(apart == 0, -4.0, near).astype(BF16)


def smooth_rows(near, f_ref, out_ref, gap_ref, diff_ref, low, high):
    _, days, width = f_ref.shape
    for e in range(low, high, BATCH):
        value = f_ref[e : e + BATCH].reshape(BATCH * days, width)
        f0, f1 = halves(value)
        lap = jnp.dot(f0, near, preferred_element_type=F32)
        lap = lap + jnp.dot(f1, near, preferred_element_type=F32)
        for k in range(BATCH):
            coef = jnp.broadcast_to(diff_ref[e + k], (CHUNK, width))
            for at in range(0, days, CHUNK):
                part = slice(at, at + CHUNK)
                around = f_ref[e + k - 1, part, :] + f_ref[e + k + 1, part, :]
                around = around + lap[k * days + at : k * days + at + CHUNK]
                out_ref[e + k, part, :] = (
                    f_ref[e + k, part, :] + (gap_ref[e + k, part, :] * coef) * around
                )


def sweep_body(sweep, last, row_of, a_ref, b_ref, seen_ref, gap_ref, diff_ref):
    total = seen_ref.shape[0]
    edge = sweep * PASSES
    project_rows(last, row_of, a_ref, seen_ref, gap_ref, edge, total - edge)
    near = beside_matrix(seen_ref.shape[2])
    now, other = a_ref, b_ref
    for step in range(PASSES):
        edge += 1
        smooth_rows(near, now, other, gap_ref, diff_ref, edge, total - edge)
        now, other = other, now
    return now


def first_kernel(*refs):
    last_ref = refs[0]
    seen, stat = refs[1:4], refs[4:7]
    west_ref, east_ref = refs[7:9]
    seen_ref, gap_ref, diff_ref, out_ref, packed_ref, a_ref = refs[9:]
    rows, days, cols = seen[1].shape
    total = rows + 2 * HALO
    side_of = lambda at, e: strip_side(rows, west_ref, east_ref, at, e)
    for e in range(total):
        seen_ref[e, :, :cols] = row_source(seen, rows, e)
        seen_ref[e, :, cols:] = side_of(slice(0, days), e)
        main, side = row_source(stat, rows, e), side_of(slice(days, None), e)
        gap_ref[e, :, :cols] = main[:days]
        gap_ref[e, :, cols:] = side[:days]
        diff_ref[e, :, :cols] = main[days : days + 1]
        diff_ref[e, :, cols:] = side[days : days + 1]
    row_of = lambda e: seen_ref[e]
    now = sweep_body(0, last_ref[...], row_of, a_ref, out_ref, seen_ref, gap_ref, diff_ref)
    assert now is out_ref
    cov = covariance_of(lambda r: out_ref[HALO + r, :, :cols], rows)
    pack_symmetric(packed_ref, cov)


def next_kernel(sweep, last_ref, f_ref, seen_ref, gap_ref, diff_ref, out_ref, packed_ref, a_ref):
    row_of = lambda e: f_ref[e]
    now = sweep_body(sweep, last_ref[...], row_of, a_ref, out_ref, seen_ref, gap_ref, diff_ref)
    assert now is out_ref
    rows, cols = out_ref.shape[0] - 2 * HALO, out_ref.shape[2] // 2
    pack_symmetric(packed_ref, covariance_of(lambda r: out_ref[HALO + r, :, :cols], rows))


def end_kernel(sweep, last_ref, f_ref, seen_ref, gap_ref, diff_ref, out_ref, a_ref, b_ref):
    row_of = lambda e: f_ref[e]
    now = sweep_body(sweep, last_ref[...], row_of, a_ref, b_ref, seen_ref, gap_ref, diff_ref)
    days, rows, cols = out_ref.shape
    flat = out_ref.reshape(days * rows, cols)
    for r in range(rows):
        flat[pl.ds(r, days, stride=rows), :] = now[HALO + r, :, :cols]


def call(kernel, name, ins, outs, scratch=(), scalars=0):
    specs = [SMEM] * scalars + [VMEM] * (len(ins) - scalars)
    return pl.pallas_call(
        kernel,
        name=name,
        out_shape=[jax.ShapeDtypeStruct(s, F32) for s in outs],
        in_specs=specs,
        out_specs=[VMEM] * len(outs),
        scratch_shapes=[pltpu.VMEM(s, F32) for s in scratch],
        compiler_params=pltpu.CompilerParams(vmem_limit_bytes=24 * 2**20),
    )(*ins)


def pair_sums(packed):
    count = lax.axis_size("band")
    width = packed.shape[2]
    parity = lax.rem(lax.axis_index("band"), 2)
    mine = lax.dynamic_slice_in_dim(packed, parity, 1, 0)
    other = lax.dynamic_slice_in_dim(packed, 1 - parity, 1, 0)
    got = lax.ppermute(other, "band", [(i, i ^ 1) for i in range(count)])
    everyone = count * lax.axis_size("wide")
    return jnp.broadcast_to(mine + got, (everyone, 1, width))


def trade(copies):
    return lax.all_to_all(copies, ("wide", "band"), 0, 0, tiled=True)


def edges(head, cells, tail):
    count = lax.axis_size("band")
    north = lax.ppermute(tail, "band", [(i, i + 1) for i in range(count - 1)])
    south = lax.ppermute(head, "band", [(i + 1, i) for i in range(count - 1)])
    return [north, cells, south]


def beside(east, west):
    count = lax.axis_size("wide")
    from_west = lax.ppermute(east, "wide", [(i, (i + 1) % count) for i in range(count)])
    from_east = lax.ppermute(west, "wide", [((i + 1) % count, i) for i in range(count)])
    return [from_west, from_east]


def shards(day_field, obs_mask, ocean_mask, diffusivity, start_modes):
    days, rows, cols = obs_mask.shape
    modes = start_modes.shape[1]
    count = lax.axis_size("wide")
    me = lax.axis_index("wide")
    pieces, offs = [], []
    for k in range(count):
        to = lambda i: i ^ k
        piece = lax.dynamic_slice_in_dim(day_field, to(me) * cols, cols, 2)
        if k:
            piece = lax.ppermute(piece, "wide", [(i, to(i)) for i in range(count)])
        pieces.append(piece)
        offs.append(to(me) * day_field.shape[0])
    offs = jnp.stack(offs).astype(jnp.int32)
    (stat,) = call(
        static_kernel, "static", [obs_mask, ocean_mask, diffusivity], [(rows, days + EXTRA, cols)]
    )
    stats = edges(stat[:HALO], stat, stat[rows - HALO :])
    (basis,) = call(start_kernel, "start", [start_modes.T], [(modes, days)])
    width = (days // 8 + 1) * LANES
    row_strip = (HALO, days, cols)
    seen, head, tail, packed = call(
        functools.partial(observed_kernel, count),
        "observed",
        [offs] + pieces + [stat, basis],
        [(rows, days, cols), row_strip, row_strip, (2, 1, width)],
        scalars=1,
    )
    seens = edges(head, seen, tail)
    total = rows + 2 * HALO
    strip = (strip_places(rows, cols)[1], 2 * days + EXTRA, cols)
    wide_map, wide_row = (total, days, 2 * cols), (total, 1, 2 * cols)
    parts = trade(pair_sums(packed))
    east, west = call(strip_kernel, "strips", seens + stats, [strip, strip])
    sides = beside(east, west)
    for sweep in range(OUTER):
        basis, last = call(
            modes_kernel,
            "modes",
            [parts, basis],
            [(modes, days), (days, days)],
            [(days // 4, LANES)],
        )
        if sweep == 0:
            seen_w, gap_w, diff_w, filled, packed = call(
                first_kernel,
                "sweep0",
                [last] + seens + stats + sides,
                [wide_map, wide_map, wide_row, wide_map, (2, 1, width)],
                [wide_map],
            )
        elif sweep < OUTER - 1:
            filled, packed = call(
                functools.partial(next_kernel, sweep),
                f"sweep{sweep}",
                [last, filled, seen_w, gap_w, diff_w],
                [wide_map, (2, 1, width)],
                [wide_map],
            )
        else:
            (out,) = call(
                functools.partial(end_kernel, sweep),
                f"sweep{sweep}",
                [last, filled, seen_w, gap_w, diff_w],
                [(days, rows, cols)],
                [wide_map, wide_map],
            )
            return (out, basis.T)
        parts = trade(pair_sums(packed))


def solution(mesh):
    placed = (
        P("wide", "band", None),
        P(None, "band", "wide"),
        P("band", "wide"),
        P("band", "wide"),
        P(),
    )
    return jax.shard_map(
        shards,
        mesh=mesh,
        in_specs=placed,
        out_specs=(P(None, "band", "wide"), P()),
        check_vma=False,
    )
```
